32 devices in a mesh: ctx: 4 (over y, x), fsdp: 8 (over z, core).
Axes of the slice: x: 2, y: 2, z: 4, core: 2. Of those that a mesh axis runs over, the one named last changes fastest.
Arguments:
- tokens: bfloat16 [8, 1024, 2048], P('fsdp', 'ctx'), may hold values from -6 to 6
- seq_ids: int32 [8, 1024], P('fsdp', 'ctx'), may hold values from 0 to 1, as said below
- positions: int32 [8, 1024], P('fsdp', 'ctx'), may hold values from 0 to 767, as said below
- ln1_gain: bfloat16 [2048], replicated, may hold values from 0.5 to 1.5
- ln1_bias: bfloat16 [2048], replicated, may hold values from -3 to 3
- ln2_gain: bfloat16 [2048], replicated, may hold values from 0.5 to 1.5
- ln2_bias: bfloat16 [2048], replicated, may hold values from -3 to 3
- w_qkv: bfloat16 [2048, 6144], P(('ctx', 'fsdp'))
- w_out: bfloat16 [2048, 2048], P(('ctx', 'fsdp')), may hold values from -2 to 2
- w_up: bfloat16 [2048, 8192], P(('ctx', 'fsdp')), may hold values from -0.125 to 0.125
- w_down: bfloat16 [2048, 8192], P(('ctx', 'fsdp')), may hold values from -0.0625 to 0.0625
- grad_out: bfloat16 [8, 1024, 2048], P('fsdp', 'ctx'), may hold values from -6 to 6
Outputs:
- output: bfloat16 [8, 1024, 2048], P('fsdp', 'ctx')
- grad_tokens: bfloat16 [8, 1024, 2048], P('fsdp', 'ctx')
- grad_ln1_gain: float32 [2048], P(('ctx', 'fsdp'))
- grad_ln1_bias: float32 [2048], P(('ctx', 'fsdp'))
- grad_ln2_gain: float32 [2048], P(('ctx', 'fsdp'))
- grad_ln2_bias: float32 [2048], P(('ctx', 'fsdp'))
- grad_w_qkv: float32 [2048, 6144], P(('ctx', 'fsdp'))
- grad_w_out: float32 [2048, 2048], P(('ctx', 'fsdp'))
- grad_w_up: float32 [2048, 8192], P(('ctx', 'fsdp'))
- grad_w_down: float32 [2048, 8192], P(('ctx', 'fsdp'))
The draws below stay inside these ranges and needn't reach their ends.
Inputs may be any that keep to these rules, and one draw needn't show every extreme that they name: `seq_ids`: in each pack the tokens of document 0 come first and those of document 1 follow; each document has 256 tokens or more. `positions`: A token's index within its document, 0 at the document's first token.
All inputs are finite; a program needn't handle non-finite values.
Results may differ from the reference program's by a relative error of at most 0.03.
Values may be sent and summed in bfloat16 or wider, within the bound.
No kernel may reach another device: no remote copies, remote signals or barrier semaphores. Data moves between devices by JAX's collectives and lax.ppermute only.
A program may use at most 768 MiB of HBM per device.

```python
import jax
import jax.numpy as jnp
from jax import lax

D = 2048
HEADS = 8
HEAD_DIM = 256
ROT = 64
FF = 8192
MINDOC = 256
SEQLEN = 1024
BLOCK = 256
GROUPS = 8
N_CTX = 4


def doc_layout(key):
    inner = jax.random.fold_in(key, 11)
    cuts = jax.random.randint(inner, (GROUPS, 1), MINDOC, SEQLEN - MINDOC + 1)
    first_row = jnp.arange(GROUPS, dtype=jnp.int32)[:, None] == 0
    cuts = jnp.where(first_row, MINDOC, cuts).astype(jnp.int32)
    index = jnp.arange(SEQLEN, dtype=jnp.int32)[None, :]
    second = (index >= cuts).astype(jnp.int32)
    return (second, index - cuts * second)


def draw_seq_ids(key, part):
    return doc_layout(key)[0]


def draw_positions(key, part):
    return doc_layout(key)[1]


def draw_w_qkv(key, part):
    base = jax.random.normal(key, (D, 3 * D), jnp.float32) * D ** (-0.5)
    return base.astype(jnp.bfloat16)


def strengthened(values, key, source, target, parts, factor):
    owner, partner = [(jnp.arange(values.shape[axis_at]) // (values.shape[axis_at] // parts)).reshape([-1 if axis == axis_at else 1 for axis in range(values.ndim)]) for axis_at in (source, target)]
    chosen = jax.random.permutation(key, parts)[partner]
    strong = (owner == chosen) | (owner == (partner + parts // 2) % parts)
    return jnp.where(strong, factor * values, values)


def level_of(stream_key, shape, split, smallest, largest):
    def one(position, shards_of):
        heights = jax.random.uniform(jax.random.fold_in(jax.random.fold_in(stream_key, 6), position), (shards_of,), jnp.float32, smallest / len(split), largest / len(split))
        return jnp.repeat(jnp.exp(heights), shape[position] // shards_of).reshape((-1,) + (1,) * (len(shape) - position - 1))

    level = one(*split[0])
    for cut in split[1:]:
        level = level * one(*cut)
    return level


def normal_values(key, dims, spread, most, shards=(), kind=jnp.bfloat16):
    values = jax.random.normal(key, dims, jnp.float32) * spread
    if len(shards) > 0:
        values = level_of(key, dims, shards, -0.22, 0.18) * values
    return jnp.clip(values, min=-most, max=most).astype(kind)


def bell_draw_with(rng, shape, width, bound, shards, heavy, held_as=jnp.bfloat16):
    array = width * jax.random.normal(rng, shape, jnp.float32)
    if shards:
        array = array * level_of(rng, shape, shards, -0.22, 0.18)
    return jnp.clip(strengthened(array, jax.random.fold_in(rng, 3), *heavy), -bound, bound).astype(held_as)


def setup_inputs(seed: int = 0) -> dict:
    splits = jax.random.split(jax.random.key(seed), 13)
    tokens = normal_values(splits[0], (GROUPS, SEQLEN, D), 1.0, 6.0, ((0, 8), (1, 4)))
    seq_ids = draw_seq_ids(jax.random.fold_in(splits[12], 71), 0)
    positions = draw_positions(jax.random.fold_in(splits[12], 71), 0)
    ln1_gain = jnp.clip(1.0 + 0.1 * jax.random.normal(splits[3], (D,), jnp.float32), 0.5, 1.5).astype(jnp.bfloat16)
    ln1_bias = normal_values(splits[4], (D,), 0.5, 3.0)
    ln2_gain = jnp.clip(1.0 + 0.1 * jax.random.normal(splits[5], (D,), jnp.float32), 0.5, 1.5).astype(jnp.bfloat16)
    ln2_bias = normal_values(splits[6], (D,), 0.5, 3.0)
    w_qkv = draw_w_qkv(jax.random.fold_in(splits[12], 71), 0)
    w_out = normal_values(splits[8], (D, D), (max(D // 256, 8)) ** -0.5, 2.0, ((0, 32),))
    w_up = normal_values(splits[9], (D, FF), D ** -0.5, 0.125, ((0, 32),))
    w_down = normal_values(splits[10], (D, FF), FF ** -0.5, 0.0625, ((0, 32),))
    grad_out = bell_draw_with(splits[11], (GROUPS, SEQLEN, D), 1.0, 6.0, ((0, 8), (1, 4)), (1, 2, 4, 2.0))
    return dict(tokens=tokens, seq_ids=seq_ids, positions=positions, ln1_gain=ln1_gain, ln1_bias=ln1_bias, ln2_gain=ln2_gain, ln2_bias=ln2_bias, w_qkv=w_qkv, w_out=w_out, w_up=w_up, w_down=w_down, grad_out=grad_out)


NORM_EPS = 1e-05
NEG_FILL = -1e+30
ROPE_BASE = 10000.0
HIGH = lax.Precision.HIGHEST

@jax.custom_vjp
def low(v):
    return lax.optimization_barrier(v.astype(jnp.bfloat16)).astype(jnp.float32)

@jax.custom_vjp
def low_back(v):
    return v

def low_keep(v):
    return (low(v), None)

def low_pass(kept, grad):
    return (grad,)

def back_keep(v):
    return (v, None)

def back_low(kept, grad):
    return (low(grad),)
low.defvjp(low_keep, low_pass)
low_back.defvjp(back_keep, back_low)

def layer_norm(inputs, gain, shift):
    row_mean = lax.optimization_barrier(jnp.mean(inputs, axis=-1, keepdims=True))
    centred = inputs - row_mean
    inv_std = lax.rsqrt(lax.optimization_barrier(jnp.mean(centred * centred, axis=-1, keepdims=True)) + NORM_EPS)
    return centred * inv_std * gain + shift

def rotary_tables(position_row):
    half_dims = ROT // 2
    freqs = ROPE_BASE ** (-(jnp.arange(half_dims, dtype=jnp.float32) * 2.0) / ROT)
    angles = position_row.astype(jnp.float32)[:, None] * freqs[None, :]
    cosines = jnp.cos(angles)
    sines = jnp.sin(angles)
    return (jnp.concatenate([cosines, cosines], -1)[:, None, :], jnp.concatenate([sines, sines], -1)[:, None, :])

def rotate(heads, cosines, sines):
    half_dims = ROT // 2
    turned = heads[..., :ROT]
    swapped = jnp.concatenate([-turned[..., half_dims:], turned[..., :half_dims]], -1)
    return jnp.concatenate([turned * cosines + swapped * sines, heads[..., ROT:]], -1)

def attend_queries(block_queries, block_seq, block_pos, keys_all, values_all, seq_row, pos_row):
    query_rows = block_queries.shape[0]
    scores = low_back(jnp.einsum('qhd,khd->hqk', block_queries, keys_all, precision=HIGH) * HEAD_DIM ** (-0.5))
    allowed = (block_seq[:, None] == seq_row[None, :]) & (pos_row[None, :] <= block_pos[:, None])
    masked = jnp.where(allowed[None], scores, NEG_FILL)
    shaped = masked.reshape(HEADS, query_rows, N_CTX, BLOCK)
    block_max = lax.optimization_barrier(jnp.max(shaped, axis=-1))
    weights = jnp.where(allowed.reshape(query_rows, N_CTX, BLOCK)[None], jnp.exp(shaped - block_max[..., None]), 0.0)
    block_total = lax.optimization_barrier(jnp.sum(weights, axis=-1))
    block_out = low_back(jnp.einsum('hqnk,nkhd->hqnd', low(weights), values_all.reshape(N_CTX, BLOCK, HEADS, HEAD_DIM), precision=HIGH))
    overall_max = lax.optimization_barrier(jnp.max(block_max, axis=-1))
    mixing = jnp.exp(block_max - overall_max[..., None])
    grand_total = lax.optimization_barrier(jnp.sum(mixing * block_total, axis=-1))
    attended = lax.optimization_barrier(jnp.sum(mixing[..., None] * block_out, axis=2)) / grand_total[..., None]
    return attended.transpose(1, 0, 2).reshape(query_rows, D)

def one_sequence(item, params):
    inputs, seq_row, pos_row = item
    gain_one, bias_one, gain_two, bias_two, weight_qkv, weight_out, weight_up, weight_down = params
    first_in = low(layer_norm(inputs, gain_one, bias_one))
    second_in = low(layer_norm(inputs, gain_two, bias_two))
    projected = low_back(jnp.dot(first_in, weight_qkv, precision=HIGH, preferred_element_type=jnp.float32))
    cosines, sines = rotary_tables(pos_row)
    queries = low(rotate(projected[:, :D].reshape(SEQLEN, HEADS, HEAD_DIM), cosines, sines))
    keys_all = low(rotate(projected[:, D:2 * D].reshape(SEQLEN, HEADS, HEAD_DIM), cosines, sines))
    values_all = low(projected[:, 2 * D:].reshape(SEQLEN, HEADS, HEAD_DIM))
    query_rows = min(512, SEQLEN)
    block_count = SEQLEN // query_rows

    def attend_part(part):
        return attend_queries(part[0], part[1], part[2], keys_all, values_all, seq_row, pos_row)
    attended = lax.map(jax.checkpoint(attend_part), (queries.reshape(block_count, query_rows, HEADS, HEAD_DIM), seq_row.reshape(block_count, query_rows), pos_row.reshape(block_count, query_rows)))
    attended = attended.reshape(SEQLEN, D)
    attn_branch = jnp.dot(low(attended), weight_out, precision=HIGH, preferred_element_type=jnp.float32)
    hidden_pre = low_back(jnp.dot(second_in, weight_up, precision=HIGH, preferred_element_type=jnp.float32))
    activated = low(jax.nn.gelu(hidden_pre, approximate=False))
    mlp_branch = jnp.dot(activated, weight_down.T, precision=HIGH, preferred_element_type=jnp.float32)
    return inputs + attn_branch + mlp_branch

def reference(tokens, seq_ids, positions, ln1_gain, ln1_bias, ln2_gain, ln2_bias, w_qkv, w_out, w_up, w_down, grad_out):

    def run(inputs, gain_one, bias_one, gain_two, bias_two, weight_qkv, weight_out, weight_up, weight_down):
        params = (gain_one, bias_one, gain_two, bias_two, weight_qkv, weight_out, weight_up, weight_down)
        return lax.map(lambda item: one_sequence(item, params), (inputs, seq_ids, positions))
    output, pull = jax.vjp(run, tokens.astype(jnp.float32), ln1_gain.astype(jnp.float32), ln1_bias.astype(jnp.float32), ln2_gain.astype(jnp.float32), ln2_bias.astype(jnp.float32), w_qkv.astype(jnp.float32), w_out.astype(jnp.float32), w_up.astype(jnp.float32), w_down.astype(jnp.float32))
    grads = pull(grad_out.astype(jnp.float32))
    return (output.astype(jnp.bfloat16), grads[0].astype(jnp.bfloat16), grads[1], grads[2], grads[3], grads[4], grads[5], grads[6], grads[7], grads[8])
```

```python
from functools import partial

import jax
import jax.numpy as jnp
from jax import lax
from jax.sharding import PartitionSpec as P

HEADS = 8
HEAD_DIM = 256
ROT = 64


NORM_EPS = 1e-05
NEG_FILL = -1e30
ROPE_BASE = 10000.0
ROWS_FIRST = (((0,), (0,)), ((), ()))
COLS_BOTH = (((1,), (1,)), ((), ()))


def swap(value, step):
    count = lax.axis_size("ctx")
    return lax.ppermute(value, "ctx", [(i, i ^ step) for i in range(count)])


def gather_ctx(block):
    count = lax.axis_size("ctx")
    return jnp.concatenate([block] + [swap(block, k) for k in range(1, count)], 0)


def scatter_ctx(parts, rows):
    count = lax.axis_size("ctx")
    low = parts.astype(jnp.bfloat16)
    total = parts[:rows]
    for k in range(1, count):
        total = total + swap(low[k * rows : (k + 1) * rows], k).astype(jnp.float32)
    return total


def normalize(inputs):
    row_mean = jnp.mean(inputs, axis=-1, keepdims=True)
    centred = inputs - row_mean
    inv_std = lax.rsqrt(jnp.mean(centred * centred, axis=-1, keepdims=True) + NORM_EPS)
    return (centred * inv_std, inv_std)


def rotary_tables(position_row):
    half_dims = ROT // 2
    freqs = ROPE_BASE ** (-(jnp.arange(half_dims, dtype=jnp.float32) * 2.0) / ROT)
    angles = position_row.astype(jnp.float32)[:, None] * freqs[None, :]
    cosines = jnp.cos(angles)
    sines = jnp.sin(angles)
    return (
        jnp.concatenate([cosines, cosines], -1)[:, None, :],
        jnp.concatenate([sines, sines], -1)[:, None, :],
    )


def rotate(heads, cosines, sines):
    half_dims = ROT // 2
    turned = heads[..., :ROT]
    swapped = jnp.concatenate([-turned[..., half_dims:], turned[..., :half_dims]], -1)
    return jnp.concatenate([turned * cosines + swapped * sines, heads[..., ROT:]], -1)


def column_slices(shard, groups):
    count = lax.axis_size("ctx")
    rows, columns = shard.shape
    split = shard.reshape(rows, groups, count, columns // (groups * count)).transpose(2, 0, 1, 3)
    split = split.reshape(count, rows, columns // count)
    mine = lax.all_to_all(split, "ctx", 0, 0, tiled=True)
    full = lax.all_gather(mine, "fsdp", axis=0, tiled=False)
    return full.transpose(1, 0, 2, 3).reshape(-1, columns // count)


def after(value, earlier):
    return value if earlier is None else lax.optimization_barrier((value, earlier))[0]


def sum_rows(grad, earlier):
    count = lax.axis_size("ctx")
    shards = lax.axis_size("fsdp")
    width, columns = grad.shape
    rows = width // (count * shards)
    split = grad.astype(jnp.bfloat16).reshape(count, shards, rows, columns).transpose(1, 0, 2, 3)
    split = after(split.reshape(width, columns), earlier)
    return lax.psum_scatter(split, "fsdp", scatter_dimension=0, tiled=True)


def row_shards(summed, groups):
    count = lax.axis_size("ctx")
    rows, columns = summed.shape[0] // count, summed.shape[1]
    mine = lax.all_to_all(summed.reshape(count, rows, columns), "ctx", 0, 0, tiled=True)
    mine = mine.reshape(count, rows, groups, columns // groups).transpose(1, 2, 0, 3)
    return mine.reshape(rows, count * columns).astype(jnp.float32)


def on_device(
    tokens,
    seq_ids,
    positions,
    ln1_gain,
    ln1_bias,
    ln2_gain,
    ln2_bias,
    w_qkv,
    w_out,
    w_up,
    w_down,
    grad_out,
):
    f32 = jnp.float32
    bf16 = jnp.bfloat16
    rows = tokens.shape[1]
    width = tokens.shape[2]
    ctx_count = lax.axis_size("ctx")
    heads = HEADS // ctx_count
    total_rows = rows * ctx_count
    scale = HEAD_DIM ** (-0.5)
    gain_one = ln1_gain.astype(f32)
    bias_one = ln1_bias.astype(f32)
    gain_two = ln2_gain.astype(f32)
    bias_two = ln2_bias.astype(f32)

    up = column_slices(w_up, 1)
    down = column_slices(w_down, 1)
    qkv = column_slices(w_qkv, 3)
    out = lax.all_gather(w_out, "fsdp", axis=0, tiled=True)

    inputs = gather_ctx(tokens[0])
    grads = gather_ctx(grad_out[0])
    layout = gather_ctx(jnp.stack([seq_ids[0], positions[0]], 1))
    seq, pos = layout[:, 0], layout[:, 1]

    normed, inv_std = normalize(inputs.astype(f32))
    first_in = (normed * gain_one + bias_one).astype(bf16)
    second_in = (normed * gain_two + bias_two).astype(bf16)

    hidden_pre = jnp.dot(second_in, up, preferred_element_type=f32)
    gelu, gelu_pull = jax.vjp(partial(jax.nn.gelu, approximate=False), hidden_pre)
    activated = gelu.astype(bf16)
    summed_down = sum_rows(
        lax.dot_general(grads, activated, ROWS_FIRST, preferred_element_type=f32), None
    )
    grad_act = jnp.dot(grads, down, preferred_element_type=f32)
    grad_hidden = gelu_pull(grad_act)[0].astype(bf16)
    summed_up = sum_rows(
        lax.dot_general(second_in, grad_hidden, ROWS_FIRST, preferred_element_type=f32), summed_down
    )
    mlp_branch = lax.dot_general(activated, down, COLS_BOTH, preferred_element_type=f32)
    grad_second = lax.dot_general(grad_hidden, up, COLS_BOTH, preferred_element_type=f32)

    projected = jnp.dot(first_in, qkv, preferred_element_type=f32)
    projected = projected.reshape(total_rows, 3, heads, HEAD_DIM)
    cosines, sines = rotary_tables(pos)
    queries = rotate(projected[:, 0], cosines, sines).astype(bf16)
    keys = rotate(projected[:, 1], cosines, sines).astype(bf16)
    values = projected[:, 2].astype(bf16)
    scores = jnp.einsum("qhd,khd->hqk", queries, keys, preferred_element_type=f32) * scale
    allowed = ((seq[:, None] == seq[None, :]) & (pos[None, :] <= pos[:, None]))[None]
    masked = jnp.where(allowed, scores, NEG_FILL)
    row_max = jnp.max(masked, axis=-1, keepdims=True)
    weights = jnp.where(allowed, jnp.exp(masked - row_max), 0.0)
    row_total = jnp.sum(weights, axis=-1, keepdims=True)
    weights = weights / row_total
    weights_low = weights.astype(bf16)
    attended = jnp.einsum("hqk,khd->qhd", weights_low, values, preferred_element_type=f32)
    attended_low = attended.reshape(total_rows, heads * HEAD_DIM).astype(bf16)
    attn_branch = jnp.dot(attended_low, out, preferred_element_type=f32)
    output = scatter_ctx(attn_branch + mlp_branch, rows)
    output = (tokens[0].astype(f32) + output).astype(bf16)[None]

    grad_attended = lax.dot_general(grads, out, COLS_BOTH, preferred_element_type=f32)
    grad_attended = grad_attended.reshape(total_rows, heads, HEAD_DIM)
    delta = jnp.sum(grad_attended * attended, axis=-1).T[..., None]
    grad_heads = grad_attended.astype(bf16)
    grad_values = jnp.einsum("hqk,qhd->khd", weights_low, grad_heads, preferred_element_type=f32)
    grad_weights = jnp.einsum("qhd,khd->hqk", grad_heads, values, preferred_element_type=f32)
    grad_scores = (weights * (grad_weights - delta)).astype(bf16)
    grad_queries = (
        jnp.einsum("hqk,khd->qhd", grad_scores, keys, preferred_element_type=f32) * scale
    )
    grad_keys = jnp.einsum("hqk,qhd->khd", grad_scores, queries, preferred_element_type=f32) * scale
    grad_projected = jnp.stack(
        [
            rotate(grad_queries, cosines, -sines),
            rotate(grad_keys, cosines, -sines),
            grad_values,
        ],
        1,
    )
    grad_projected = grad_projected.reshape(total_rows, 3 * heads * HEAD_DIM).astype(bf16)
    summed_qkv = sum_rows(
        lax.dot_general(first_in, grad_projected, ROWS_FIRST, preferred_element_type=f32), summed_up
    )
    out_part = lax.dot_general(attended_low, grads, ROWS_FIRST, preferred_element_type=f32)
    grad_w_out = lax.psum_scatter(
        after(out_part.astype(bf16), summed_qkv), "fsdp", scatter_dimension=0, tiled=True
    ).astype(f32)
    grad_first = lax.dot_general(grad_projected, qkv, COLS_BOTH, preferred_element_type=f32)

    norm_terms = jnp.stack(
        [
            jnp.sum(grad_first * normed, 0),
            jnp.sum(grad_first, 0),
            jnp.sum(grad_second * normed, 0),
            jnp.sum(grad_second, 0),
        ]
    )
    norm_sums = lax.psum_scatter(norm_terms, ("ctx", "fsdp"), scatter_dimension=1, tiled=True)

    scaled = scatter_ctx(grad_first * gain_one + grad_second * gain_two, rows)
    own_normed = normed[:rows]
    first_mean = jnp.mean(scaled, axis=-1, keepdims=True)
    second_mean = jnp.mean(scaled * own_normed, axis=-1, keepdims=True)
    back = (scaled - first_mean - own_normed * second_mean) * inv_std[:rows]
    grad_tokens = (grad_out[0].astype(f32) + back).astype(bf16)[None]
    return (
        output,
        grad_tokens,
        norm_sums[0],
        norm_sums[1],
        norm_sums[2],
        norm_sums[3],
        row_shards(summed_qkv, 3),
        grad_w_out,
        row_shards(summed_up, 1),
        row_shards(summed_down, 1),
    )


def solution(mesh):
    return jax.shard_map(
        on_device,
        mesh=mesh,
        in_specs=(
            P("fsdp", "ctx", None),
            P("fsdp", "ctx"),
            P("fsdp", "ctx"),
            P(),
            P(),
            P(),
            P(),
            P(("ctx", "fsdp"), None),
            P(("ctx", "fsdp"), None),
            P(("ctx", "fsdp"), None),
            P(("ctx", "fsdp"), None),
            P("fsdp", "ctx", None),
        ),
        out_specs=(
            P("fsdp", "ctx", None),
            P("fsdp", "ctx", None),
            P(("ctx", "fsdp")),
            P(("ctx", "fsdp")),
            P(("ctx", "fsdp")),
            P(("ctx", "fsdp")),
            P(("ctx", "fsdp"), None),
            P(("ctx", "fsdp"), None),
            P(("ctx", "fsdp"), None),
            P(("ctx", "fsdp"), None),
        ),
        check_vma=False,
    )
```

```python
import jax
import jax.numpy as jnp
import numpy as np
from jax import lax
from jax.sharding import Mesh
from jax.sharding import PartitionSpec as P

HEADS = 8
HEAD_DIM = 256
ROT = 64


NORM_EPS = 1e-05
NEG_FILL = -1e30
ROPE_BASE = 10000.0
CORES = 2
FSDP = ("line", "core")
ROWS_FIRST = (((0,), (0,)), ((), ()))
COLS_BOTH = (((1,), (1,)), ((), ()))


def swap(value, step):
    count = lax.axis_size("ctx")
    return lax.ppermute(value, "ctx", [(i, i ^ step) for i in range(count)])


def gather_ctx(block):
    count = lax.axis_size("ctx")
    return jnp.concatenate([block] + [swap(block, k) for k in range(1, count)], 0)


def scatter_ctx(parts, rows):
    count = lax.axis_size("ctx")
    low = parts.astype(jnp.bfloat16)
    total = parts[:rows]
    for k in range(1, count):
        total = total + swap(low[k * rows : (k + 1) * rows], k).astype(jnp.float32)
    return total


def turn(value, first, second):
    lead, width = value.shape[:-1], value.shape[-1]
    split = value.reshape(*lead, first, second, width // (first * second))
    return jnp.swapaxes(split, -3, -2).reshape(*lead, width)


def normalize(inputs):
    row_mean = jnp.mean(inputs, axis=-1, keepdims=True)
    centred = inputs - row_mean
    inv_std = lax.rsqrt(jnp.mean(centred * centred, axis=-1, keepdims=True) + NORM_EPS)
    return (centred * inv_std, inv_std)


def rotary_tables(position_row):
    half_dims = ROT // 2
    freqs = ROPE_BASE ** (-(jnp.arange(half_dims, dtype=jnp.float32) * 2.0) / ROT)
    angles = position_row.astype(jnp.float32)[:, None] * freqs[None, :]
    cosines = jnp.cos(angles)
    sines = jnp.sin(angles)
    return (
        jnp.concatenate([cosines, cosines], -1)[:, None, :],
        jnp.concatenate([sines, sines], -1)[:, None, :],
    )


def rotate(heads, cosines, sines):
    half_dims = ROT // 2
    turned = heads[..., :ROT]
    swapped = jnp.concatenate([-turned[..., half_dims:], turned[..., :half_dims]], -1)
    return jnp.concatenate([turned * cosines + swapped * sines, heads[..., ROT:]], -1)


def after(value, earlier):
    return value if earlier is None else lax.optimization_barrier((value, earlier))[0]


def exchange_columns(shard, groups, earlier=None):
    count = lax.axis_size("ctx")
    rows, columns = shard.shape
    split = shard.reshape(rows, groups, count, columns // (groups * count)).transpose(2, 0, 1, 3)
    split = after(split.reshape(count, rows, columns // count), earlier)
    mine = lax.all_to_all(split, "ctx", 0, 0, tiled=True)
    return mine.reshape(count * rows, columns // count)


def gather_rows(mine):
    return lax.all_gather(mine, FSDP, axis=0, tiled=True)


def sum_pair(left, right):
    core = lax.axis_index("core")
    grad = lax.dot_general(left, right, ROWS_FIRST, preferred_element_type=jnp.float32)
    blocks = grad.astype(jnp.bfloat16).reshape(lax.axis_size("line"), CORES, -1, grad.shape[1])
    sent = lax.dynamic_index_in_dim(blocks, CORES - 1 - core, 1, keepdims=False)
    came = lax.ppermute(sent, "core", [(0, 1), (1, 0)])
    kept = lax.dynamic_index_in_dim(blocks, core, 1, keepdims=False)
    pair = kept.astype(jnp.float32) + came.astype(jnp.float32)
    return pair.astype(jnp.bfloat16).reshape(-1, grad.shape[1])


def sum_rows(pair):
    return lax.psum_scatter(pair, "line", scatter_dimension=0, tiled=True)


def fold(value, blocks, count):
    rows, columns = value.shape
    split = value.reshape(blocks, rows // blocks, count, columns // count)
    return jnp.swapaxes(split, 1, 2).reshape(rows * count, columns // count)


def unfold(value, blocks, count):
    rows, columns = value.shape
    split = value.reshape(blocks, count, rows // (blocks * count), columns)
    return jnp.swapaxes(split, 1, 2).reshape(rows // count, columns * count)


def return_columns(summed, groups):
    count = lax.axis_size("ctx")
    rows, columns = summed.shape[0] // count, summed.shape[1]
    mine = lax.all_to_all(summed.reshape(count, rows, columns), "ctx", 0, 0, tiled=True)
    part = columns // groups
    pieces = [mine[c, :, g * part : (g + 1) * part] for g in range(groups) for c in range(count)]
    return jnp.concatenate(pieces, 1).astype(jnp.float32)


def on_device(
    tokens,
    seq_ids,
    positions,
    ln1_gain,
    ln1_bias,
    ln2_gain,
    ln2_bias,
    w_qkv,
    w_out,
    w_up,
    w_down,
    grad_out,
):
    f32 = jnp.float32
    bf16 = jnp.bfloat16
    rows = tokens.shape[1]
    ctx_count = lax.axis_size("ctx")
    fsdp_count = lax.axis_size("line") * CORES
    heads = HEADS // ctx_count
    total_rows = rows * ctx_count
    scale = HEAD_DIM ** (-0.5)

    def inner(value):
        return turn(value, ctx_count, fsdp_count)

    def outer(value):
        return turn(value, fsdp_count, ctx_count)

    out = inner(gather_rows(w_out))
    mine_qkv = exchange_columns(w_qkv, 3)
    qkv = gather_rows(mine_qkv)
    mine_up = exchange_columns(w_up, 1, mine_qkv)
    up = gather_rows(mine_up)

    gain_one = inner(ln1_gain.astype(f32))
    bias_one = inner(ln1_bias.astype(f32))
    gain_two = inner(ln2_gain.astype(f32))
    bias_two = inner(ln2_bias.astype(f32))
    own_tokens = inner(tokens[0])
    own_grads = inner(grad_out[0])
    inputs = gather_ctx(after(own_tokens, mine_up))
    layout = gather_ctx(after(jnp.stack([seq_ids[0], positions[0]], 0)[None], mine_up))
    mine_down = exchange_columns(w_down, 1, inputs)
    down = gather_rows(mine_down)
    grads = gather_ctx(after(own_grads, mine_down))
    seq = layout[:, 0].reshape(-1)
    pos = layout[:, 1].reshape(-1)

    normed, inv_std = normalize(inputs.astype(f32))
    first_in = (normed * gain_one + bias_one).astype(bf16)
    second_in = (normed * gain_two + bias_two).astype(bf16)

    projected = jnp.dot(first_in, qkv, preferred_element_type=f32)
    projected = projected.reshape(total_rows, 3, heads, HEAD_DIM)
    cosines, sines = rotary_tables(pos)
    queries = rotate(projected[:, 0], cosines, sines).astype(bf16)
    keys = rotate(projected[:, 1], cosines, sines).astype(bf16)
    values = projected[:, 2].astype(bf16)
    scores = jnp.einsum("qhd,khd->hqk", queries, keys, preferred_element_type=f32) * scale
    allowed = ((seq[:, None] == seq[None, :]) & (pos[None, :] <= pos[:, None]))[None]
    masked = jnp.where(allowed, scores, NEG_FILL)
    row_max = jnp.max(masked, axis=-1, keepdims=True)
    weights = jnp.where(allowed, jnp.exp(masked - row_max), 0.0)
    row_total = jnp.sum(weights, axis=-1, keepdims=True)
    weights = weights / row_total
    weights_low = weights.astype(bf16)
    attended = jnp.einsum("hqk,khd->qhd", weights_low, values, preferred_element_type=f32)
    attended_low = attended.reshape(total_rows, heads * HEAD_DIM).astype(bf16)
    branches = jnp.dot(attended_low, out, preferred_element_type=f32)

    grad_attended = lax.dot_general(grads, out, COLS_BOTH, preferred_element_type=f32)
    grad_attended = grad_attended.reshape(total_rows, heads, HEAD_DIM)
    delta = jnp.sum(grad_attended * attended, axis=-1).T[..., None]
    grad_heads = grad_attended.astype(bf16)
    grad_values = jnp.einsum("hqk,qhd->khd", weights_low, grad_heads, preferred_element_type=f32)
    grad_weights = jnp.einsum("qhd,khd->hqk", grad_heads, values, preferred_element_type=f32)
    grad_scores = (weights * (grad_weights - delta)).astype(bf16)
    grad_queries = (
        jnp.einsum("hqk,khd->qhd", grad_scores, keys, preferred_element_type=f32) * scale
    )
    grad_keys = jnp.einsum("hqk,qhd->khd", grad_scores, queries, preferred_element_type=f32) * scale
    grad_projected = jnp.stack(
        [
            rotate(grad_queries, cosines, -sines),
            rotate(grad_keys, cosines, -sines),
            grad_values,
        ],
        1,
    )
    grad_projected = grad_projected.reshape(total_rows, 3 * heads * HEAD_DIM).astype(bf16)
    pair_qkv = sum_pair(first_in, grad_projected)
    pair_out = sum_pair(attended_low, grads)
    lines = lax.axis_size("line")
    pair_attn = jnp.concatenate([pair_qkv, fold(pair_out, lines, ctx_count)], 1)
    summed_attn = sum_rows(pair_attn)
    summed_qkv = summed_attn[:, : qkv.shape[1]]
    summed_out = unfold(summed_attn[:, qkv.shape[1] :], 1, ctx_count)
    up = after(up, pair_attn)
    grad_first = lax.dot_general(grad_projected, qkv, COLS_BOTH, preferred_element_type=f32)

    hidden_pre = jnp.dot(second_in, up, preferred_element_type=f32)
    below = 0.5 + 0.5 * lax.erf(hidden_pre * (0.5**0.5))
    bell = jnp.exp(-0.5 * hidden_pre * hidden_pre) * (0.5 / jnp.pi) ** 0.5
    activated, slope = lax.optimization_barrier(
        ((hidden_pre * below).astype(bf16), below + hidden_pre * bell)
    )
    summed_down = sum_rows(sum_pair(grads, activated))
    grad_act = jnp.dot(grads, down, preferred_element_type=f32)
    grad_hidden = (grad_act * slope).astype(bf16)
    summed_up = sum_rows(sum_pair(second_in, grad_hidden))
    branches = branches + lax.dot_general(activated, down, COLS_BOTH, preferred_element_type=f32)
    grad_second = lax.dot_general(grad_hidden, up, COLS_BOTH, preferred_element_type=f32)

    output = scatter_ctx(branches, rows) + own_tokens.astype(f32)
    output = outer(output.astype(bf16))[None]

    norm_terms = jnp.stack(
        [
            jnp.sum(grad_first * normed, 0),
            jnp.sum(grad_first, 0),
            jnp.sum(grad_second * normed, 0),
            jnp.sum(grad_second, 0),
        ]
    )
    norm_terms = norm_terms.reshape(4, fsdp_count, ctx_count, -1).transpose(2, 1, 0, 3)
    norm_terms = norm_terms.reshape(ctx_count * fsdp_count, -1)
    norm_sums = lax.all_to_all(norm_terms, ("ctx", *FSDP), 0, 0, tiled=True)
    norm_sums = jnp.sum(norm_sums, 0).reshape(4, -1)

    scaled = scatter_ctx(grad_first * gain_one + grad_second * gain_two, rows)
    own_normed = normed[:rows]
    first_mean = jnp.mean(scaled, axis=-1, keepdims=True)
    second_mean = jnp.mean(scaled * own_normed, axis=-1, keepdims=True)
    back = (scaled - first_mean - own_normed * second_mean) * inv_std[:rows]
    grad_tokens = outer((own_grads.astype(f32) + back).astype(bf16))[None]
    return (
        output,
        grad_tokens,
        norm_sums[0],
        norm_sums[1],
        norm_sums[2],
        norm_sums[3],
        return_columns(summed_qkv, 3),
        outer(summed_out.astype(f32)),
        return_columns(summed_up, 1),
        return_columns(summed_down, 1),
    )


def solution(mesh):
    shape = (mesh.shape["ctx"], mesh.shape["fsdp"] // CORES, CORES)
    split = Mesh(np.asarray(mesh.devices).reshape(shape), ("ctx", *FSDP))
    blocks = P(FSDP, "ctx", None)
    ids = P(FSDP, "ctx")
    shards = P(("ctx", *FSDP), None)
    vector = P(("ctx", *FSDP))

    return jax.shard_map(
        on_device,
        mesh=split,
        in_specs=(blocks, ids, ids, P(), P(), P(), P(), shards, shards, shards, shards, blocks),
        out_specs=(blocks, blocks, vector, vector, vector, vector, shards, shards, shards, shards),
        check_vma=False,
    )
```

```python
import jax
import jax.numpy as jnp
import numpy as np
from jax import lax
from jax.sharding import Mesh
from jax.sharding import PartitionSpec as P

HEADS = 8
HEAD_DIM = 256
ROT = 64


NORM_EPS = 1e-05
NEG_FILL = -1e30
ROPE_BASE = 10000.0
CORES = 2
FSDP = ("line", "core")
ROWS_FIRST = (((0,), (0,)), ((), ()))
COLS_BOTH = (((1,), (1,)), ((), ()))


def swap(value, step):
    count = lax.axis_size("ctx")
    return lax.ppermute(value, "ctx", [(i, i ^ step) for i in range(count)])


def blocks_of_ctx(block):
    count = lax.axis_size("ctx")
    return (block, *(swap(block, k) for k in range(1, count)))


def scatter_ctx(low, rows, until):
    count = lax.axis_size("ctx")
    came = [swap(low[k * rows : (k + 1) * rows], k) for k in range(1, count)]
    came = after(tuple(came), until)
    total = low[:rows].astype(jnp.float32)
    for part in came:
        total = total + part.astype(jnp.float32)
    return total


def turn(value, first, second):
    lead, width = value.shape[:-1], value.shape[-1]
    split = value.reshape(*lead, first, second, width // (first * second))
    return jnp.swapaxes(split, -3, -2).reshape(*lead, width)


def normalize(inputs):
    row_mean = jnp.mean(inputs, axis=-1, keepdims=True)
    centred = inputs - row_mean
    inv_std = lax.rsqrt(jnp.mean(centred * centred, axis=-1, keepdims=True) + NORM_EPS)
    return (centred * inv_std, inv_std)


def rotary_tables(position_row):
    half_dims = ROT // 2
    freqs = ROPE_BASE ** (-(jnp.arange(half_dims, dtype=jnp.float32) * 2.0) / ROT)
    angles = position_row.astype(jnp.float32)[:, None] * freqs[None, :]
    cosines = jnp.cos(angles)
    sines = jnp.sin(angles)
    return (
        jnp.concatenate([cosines, cosines], -1)[:, None, :],
        jnp.concatenate([sines, sines], -1)[:, None, :],
    )


def rotate(heads, cosines, sines):
    half_dims = ROT // 2
    turned = heads[..., :ROT]
    swapped = jnp.concatenate([-turned[..., half_dims:], turned[..., :half_dims]], -1)
    return jnp.concatenate([turned * cosines + swapped * sines, heads[..., ROT:]], -1)


def after(value, earlier):
    return value if earlier is None else lax.optimization_barrier((value, earlier))[0]


def exchange_columns(shard, groups, earlier=None):
    count = lax.axis_size("ctx")
    rows, columns = shard.shape
    split = shard.reshape(rows, groups, count, columns // (groups * count)).transpose(2, 0, 1, 3)
    split = after(split.reshape(count, rows, columns // count), earlier)
    mine = lax.all_to_all(split, "ctx", 0, 0, tiled=True)
    return mine.reshape(count * rows, columns // count)


def gather_rows(mine):
    return lax.all_gather(mine, FSDP, axis=0, tiled=True)


def sum_pair(left, right):
    core = lax.axis_index("core")
    grad = lax.dot_general(left, right, ROWS_FIRST, preferred_element_type=jnp.float32)
    blocks = grad.astype(jnp.bfloat16).reshape(lax.axis_size("line"), CORES, -1, grad.shape[1])
    sent = lax.dynamic_index_in_dim(blocks, CORES - 1 - core, 1, keepdims=False)
    came = lax.ppermute(sent, "core", [(0, 1), (1, 0)])
    kept = lax.dynamic_index_in_dim(blocks, core, 1, keepdims=False)
    pair = kept.astype(jnp.float32) + came.astype(jnp.float32)
    return pair.astype(jnp.bfloat16).reshape(-1, grad.shape[1])


def sum_rows(pair):
    return lax.psum_scatter(pair, "line", scatter_dimension=0, tiled=True)


def fold(value, blocks, count):
    rows, columns = value.shape
    split = value.reshape(blocks, rows // blocks, count, columns // count)
    return jnp.swapaxes(split, 1, 2).reshape(rows * count, columns // count)


def unfold(value, blocks, count):
    rows, columns = value.shape
    split = value.reshape(blocks, count, rows // (blocks * count), columns)
    return jnp.swapaxes(split, 1, 2).reshape(rows // count, columns * count)


def return_columns(summed, groups):
    count = lax.axis_size("ctx")
    rows, columns = summed.shape[0] // count, summed.shape[1]
    mine = lax.all_to_all(summed.reshape(count, rows, columns), "ctx", 0, 0, tiled=True)
    part = columns // groups
    pieces = [mine[c, :, g * part : (g + 1) * part] for g in range(groups) for c in range(count)]
    return jnp.concatenate(pieces, 1).astype(jnp.float32)


def on_device(
    tokens,
    seq_ids,
    positions,
    ln1_gain,
    ln1_bias,
    ln2_gain,
    ln2_bias,
    w_qkv,
    w_out,
    w_up,
    w_down,
    grad_out,
):
    f32 = jnp.float32
    bf16 = jnp.bfloat16
    rows = tokens.shape[1]
    ctx_count = lax.axis_size("ctx")
    fsdp_count = lax.axis_size("line") * CORES
    heads = HEADS // ctx_count
    total_rows = rows * ctx_count
    scale = HEAD_DIM ** (-0.5)

    def inner(value):
        return turn(value, ctx_count, fsdp_count)

    def outer(value):
        return turn(value, fsdp_count, ctx_count)

    out = inner(gather_rows(w_out))
    mine_qkv = exchange_columns(w_qkv, 3)
    qkv = gather_rows(mine_qkv)
    mine_mlp = exchange_columns(jnp.concatenate([w_up, w_down], 1), 2, mine_qkv)
    mlp = gather_rows(mine_mlp)

    gain_one = inner(ln1_gain.astype(f32))
    bias_one = inner(ln1_bias.astype(f32))
    gain_two = inner(ln2_gain.astype(f32))
    bias_two = inner(ln2_bias.astype(f32))
    own_tokens = inner(tokens[0])
    own_grads = inner(grad_out[0])
    inputs = jnp.concatenate(blocks_of_ctx(after(own_tokens, mine_mlp)), 0)
    layout = after(jnp.stack([seq_ids[0], positions[0]], 0)[None], mine_mlp)
    layout = jnp.concatenate(blocks_of_ctx(layout), 0)
    grad_blocks = blocks_of_ctx(after(own_grads, inputs))
    seq = layout[:, 0].reshape(-1)
    pos = layout[:, 1].reshape(-1)

    inputs, out = lax.optimization_barrier((inputs, out))
    normed, inv_std = normalize(inputs.astype(f32))
    first_in = (normed * gain_one + bias_one).astype(bf16)
    second_in = (normed * gain_two + bias_two).astype(bf16)

    projected = jnp.dot(first_in, qkv, preferred_element_type=f32)
    grads = jnp.concatenate(after(grad_blocks, projected), 0)
    projected = projected.reshape(total_rows, 3, heads, HEAD_DIM)
    cosines, sines = rotary_tables(pos)
    queries = rotate(projected[:, 0], cosines, sines).astype(bf16)
    keys = rotate(projected[:, 1], cosines, sines).astype(bf16)
    values = projected[:, 2].astype(bf16)
    scores = jnp.einsum("qhd,khd->hqk", queries, keys, preferred_element_type=f32) * scale
    allowed = ((seq[:, None] == seq[None, :]) & (pos[None, :] <= pos[:, None]))[None]
    masked = jnp.where(allowed, scores, NEG_FILL)
    row_max = jnp.max(masked, axis=-1, keepdims=True)
    weights = jnp.where(allowed, jnp.exp(masked - row_max), 0.0)
    row_total = jnp.sum(weights, axis=-1, keepdims=True)
    weights = weights / row_total
    weights_low = weights.astype(bf16)
    attended = jnp.einsum("hqk,khd->qhd", weights_low, values, preferred_element_type=f32)
    attended_low = attended.reshape(total_rows, heads * HEAD_DIM).astype(bf16)

    grad_attended = lax.dot_general(grads, out, COLS_BOTH, preferred_element_type=f32)
    grad_attended = grad_attended.reshape(total_rows, heads, HEAD_DIM)
    delta = jnp.sum(grad_attended * attended, axis=-1).T[..., None]
    grad_heads = grad_attended.astype(bf16)
    grad_values = jnp.einsum("hqk,qhd->khd", weights_low, grad_heads, preferred_element_type=f32)
    grad_weights = jnp.einsum("qhd,khd->hqk", grad_heads, values, preferred_element_type=f32)
    grad_scores = (weights * (grad_weights - delta)).astype(bf16)
    grad_queries = (
        jnp.einsum("hqk,khd->qhd", grad_scores, keys, preferred_element_type=f32) * scale
    )
    grad_keys = jnp.einsum("hqk,qhd->khd", grad_scores, queries, preferred_element_type=f32) * scale
    grad_projected = jnp.stack(
        [
            rotate(grad_queries, cosines, -sines),
            rotate(grad_keys, cosines, -sines),
            grad_values,
        ],
        1,
    )
    grad_projected = grad_projected.reshape(total_rows, 3 * heads * HEAD_DIM).astype(bf16)
    pair_qkv = sum_pair(first_in, grad_projected)
    pair_out = sum_pair(attended_low, grads)
    lines = lax.axis_size("line")
    pair_attn = jnp.concatenate([pair_qkv, fold(pair_out, lines, ctx_count)], 1)
    summed_attn = sum_rows(pair_attn)
    mlp = after(mlp, pair_attn)
    half = mlp.shape[1] // 2
    up = mlp[:, :half]

    hidden_pre = jnp.dot(second_in, up, preferred_element_type=f32)
    below = 0.5 + 0.5 * lax.erf(hidden_pre * (0.5**0.5))
    bell = jnp.exp(-0.5 * hidden_pre * hidden_pre) * (0.5 / jnp.pi) ** 0.5
    active = (hidden_pre * below).astype(bf16)
    slope = below + hidden_pre * bell
    activated, slope = lax.optimization_barrier((active, slope))
    pair_down = sum_pair(grads, activated)
    summed_down = sum_rows(pair_down)
    mlp = after(mlp, pair_down)
    grad_act = jnp.dot(grads, mlp[:, half:], preferred_element_type=f32)
    grad_hidden = (grad_act * slope).astype(bf16)
    branches = jnp.dot(attended_low, out, preferred_element_type=f32)
    down_part = lax.dot_general(
        activated, mlp[:, half:], COLS_BOTH, preferred_element_type=f32
    )
    branches = (branches + down_part).astype(bf16)
    grad_hidden = after(grad_hidden, branches)
    pair_up = sum_pair(second_in, grad_hidden)
    summed_up = sum_rows(pair_up)
    output = scatter_ctx(branches, rows, pair_up) + own_tokens.astype(f32)
    output = outer(output.astype(bf16))[None]

    mlp, qkv, summed_attn = lax.optimization_barrier((mlp, qkv, summed_attn, pair_up))[:3]
    summed_qkv = summed_attn[:, : qkv.shape[1]]
    summed_out = unfold(summed_attn[:, qkv.shape[1] :], 1, ctx_count)
    grad_second = lax.dot_general(grad_hidden, mlp[:, :half], COLS_BOTH, preferred_element_type=f32)
    grad_first = lax.dot_general(grad_projected, qkv, COLS_BOTH, preferred_element_type=f32)
    scaled = (grad_first * gain_one + grad_second * gain_two).astype(bf16)
    grad_first, grad_second, scaled = lax.optimization_barrier((grad_first, grad_second, scaled))
    norm_terms = jnp.stack(
        [
            jnp.sum(grad_first * normed, 0),
            jnp.sum(grad_first, 0),
            jnp.sum(grad_second * normed, 0),
            jnp.sum(grad_second, 0),
        ]
    )
    scaled = scatter_ctx(scaled, rows, norm_terms)
    norm_terms = norm_terms.reshape(4, fsdp_count, ctx_count, -1).transpose(2, 1, 0, 3)
    norm_terms = norm_terms.reshape(ctx_count * fsdp_count, -1)
    norm_sums = lax.all_to_all(norm_terms, ("ctx", *FSDP), 0, 0, tiled=True)
    norm_sums = jnp.sum(norm_sums, 0).reshape(4, -1)

    own_normed = normed[:rows]
    first_mean = jnp.mean(scaled, axis=-1, keepdims=True)
    second_mean = jnp.mean(scaled * own_normed, axis=-1, keepdims=True)
    back = (scaled - first_mean - own_normed * second_mean) * inv_std[:rows]
    grad_tokens = outer((own_grads.astype(f32) + back).astype(bf16))[None]
    return (
        output,
        grad_tokens,
        norm_sums[0],
        norm_sums[1],
        norm_sums[2],
        norm_sums[3],
        return_columns(summed_qkv, 3),
        outer(summed_out.astype(f32)),
        return_columns(summed_up, 1),
        return_columns(summed_down, 1),
    )


def solution(mesh):
    shape = (mesh.shape["ctx"], mesh.shape["fsdp"] // CORES, CORES)
    split = Mesh(np.asarray(mesh.devices).reshape(shape), ("ctx", *FSDP))
    blocks = P(FSDP, "ctx", None)
    ids = P(FSDP, "ctx")
    shards = P(("ctx", *FSDP), None)
    vector = P(("ctx", *FSDP))

    return jax.shard_map(
        on_device,
        mesh=split,
        in_specs=(blocks, ids, ids, P(), P(), P(), P(), shards, shards, shards, shards, blocks),
        out_specs=(blocks, blocks, vector, vector, vector, vector, shards, shards, shards, shards),
        check_vma=False,
    )
```

```python
import jax
import jax.numpy as jnp
import numpy as np
from jax import lax
from jax.sharding import Mesh
from jax.sharding import PartitionSpec as P

HEADS = 8
HEAD_DIM = 256
ROT = 64


NORM_EPS = 1e-05
NEG_FILL = -1e30
ROPE_BASE = 10000.0
CORES = 2
FSDP = ("line", "core")
ROWS_FIRST = (((0,), (0,)), ((), ()))
COLS_BOTH = (((1,), (1,)), ((), ()))


def swap(value, step):
    count = lax.axis_size("ctx")
    return lax.ppermute(value, "ctx", [(i, i ^ step) for i in range(count)])


def blocks_of_ctx(block):
    count = lax.axis_size("ctx")
    return (block, *(swap(block, k) for k in range(1, count)))


def scatter_ctx(low, rows, until):
    count = lax.axis_size("ctx")
    came = [swap(low[k * rows : (k + 1) * rows], k) for k in range(1, count)]
    came = after(tuple(came), until)
    total = low[:rows].astype(jnp.float32)
    for part in came:
        total = total + part.astype(jnp.float32)
    return total


def turn(value, first, second):
    lead, width = value.shape[:-1], value.shape[-1]
    split = value.reshape(*lead, first, second, width // (first * second))
    return jnp.swapaxes(split, -3, -2).reshape(*lead, width)


def normalize(inputs):
    row_mean = jnp.mean(inputs, axis=-1, keepdims=True)
    centred = inputs - row_mean
    inv_std = lax.rsqrt(jnp.mean(centred * centred, axis=-1, keepdims=True) + NORM_EPS)
    return (centred * inv_std, inv_std)


def rotary_tables(position_row):
    half_dims = ROT // 2
    freqs = ROPE_BASE ** (-(jnp.arange(half_dims, dtype=jnp.float32) * 2.0) / ROT)
    angles = position_row.astype(jnp.float32)[:, None] * freqs[None, :]
    cosines = jnp.cos(angles)
    sines = jnp.sin(angles)
    return (
        jnp.concatenate([cosines, cosines], -1)[:, None, :],
        jnp.concatenate([sines, sines], -1)[:, None, :],
    )


def rotate(heads, cosines, sines):
    half_dims = ROT // 2
    turned = heads[..., :ROT]
    swapped = jnp.concatenate([-turned[..., half_dims:], turned[..., :half_dims]], -1)
    return jnp.concatenate([turned * cosines + swapped * sines, heads[..., ROT:]], -1)


def after(value, earlier):
    return value if earlier is None else lax.optimization_barrier((value, earlier))[0]


def exchange_columns(shard, groups, earlier=None):
    count = lax.axis_size("ctx")
    rows, columns = shard.shape
    split = shard.reshape(rows, groups, count, columns // (groups * count)).transpose(2, 0, 1, 3)
    split = after(split.reshape(count, rows, columns // count), earlier)
    mine = lax.all_to_all(split, "ctx", 0, 0, tiled=True)
    return mine.reshape(count * rows, columns // count)


def gather_rows(mine):
    return lax.all_gather(mine, FSDP, axis=0, tiled=True)


def sum_pair(left, right):
    core = lax.axis_index("core")
    grad = lax.dot_general(left, right, ROWS_FIRST, preferred_element_type=jnp.float32)
    blocks = grad.astype(jnp.bfloat16).reshape(lax.axis_size("line"), CORES, -1, grad.shape[1])
    sent = lax.dynamic_index_in_dim(blocks, CORES - 1 - core, 1, keepdims=False)
    came = lax.ppermute(sent, "core", [(0, 1), (1, 0)])
    kept = lax.dynamic_index_in_dim(blocks, core, 1, keepdims=False)
    pair = kept.astype(jnp.float32) + came.astype(jnp.float32)
    return pair.astype(jnp.bfloat16).reshape(-1, grad.shape[1])


def sum_rows(pair):
    return lax.psum_scatter(pair, "line", scatter_dimension=0, tiled=True)


def fold(value, blocks, count):
    rows, columns = value.shape
    split = value.reshape(blocks, rows // blocks, count, columns // count)
    return jnp.swapaxes(split, 1, 2).reshape(rows * count, columns // count)


def unfold(value, blocks, count):
    rows, columns = value.shape
    split = value.reshape(blocks, count, rows // (blocks * count), columns)
    return jnp.swapaxes(split, 1, 2).reshape(rows // count, columns * count)


def return_columns(summed, groups, until):
    count = lax.axis_size("ctx")
    split = summed.reshape(count, summed.shape[0] // count, summed.shape[1])
    mine = lax.all_to_all(split, "ctx", 0, 0, tiled=True)
    return row_shard(after(mine, until), groups)


def return_early(pair):
    count, lines = lax.axis_size("ctx"), lax.axis_size("line")
    split = pair.reshape(lines, count, -1, pair.shape[1]).swapaxes(0, 1)
    return lax.all_to_all(split, "ctx", 0, 0, tiled=True)


def row_shard(mine, groups):
    if groups > 1:
        split = mine.reshape(*mine.shape[:2], groups, -1).transpose(1, 2, 0, 3)
        return split.reshape(mine.shape[1], -1).astype(jnp.float32)
    part = mine.shape[2] // groups
    pieces = [
        mine[c, :, g * part : (g + 1) * part] for g in range(groups) for c in range(mine.shape[0])
    ]
    return jnp.concatenate(pieces, 1).astype(jnp.float32)


def on_device(
    tokens,
    seq_ids,
    positions,
    ln1_gain,
    ln1_bias,
    ln2_gain,
    ln2_bias,
    w_qkv,
    w_out,
    w_up,
    w_down,
    grad_out,
):
    f32 = jnp.float32
    bf16 = jnp.bfloat16
    rows = tokens.shape[1]
    ctx_count = lax.axis_size("ctx")
    fsdp_count = lax.axis_size("line") * CORES
    heads = HEADS // ctx_count
    total_rows = rows * ctx_count
    scale = HEAD_DIM ** (-0.5)

    def inner(value):
        return turn(value, ctx_count, fsdp_count)

    def outer(value):
        return turn(value, fsdp_count, ctx_count)

    out = inner(gather_rows(w_out))
    mine_qkv = exchange_columns(w_qkv, 3)
    qkv = gather_rows(mine_qkv)
    mine_mlp = exchange_columns(jnp.concatenate([w_up, w_down], 1), 2, mine_qkv)
    mlp = gather_rows(mine_mlp)

    gain_one = inner(ln1_gain.astype(f32))
    bias_one = inner(ln1_bias.astype(f32))
    gain_two = inner(ln2_gain.astype(f32))
    bias_two = inner(ln2_bias.astype(f32))
    own_tokens = inner(tokens[0])
    own_grads = inner(grad_out[0])
    inputs = jnp.concatenate(blocks_of_ctx(after(own_tokens, mine_mlp)), 0)
    layout = after(jnp.stack([seq_ids[0], positions[0]], 0)[None], mine_mlp)
    layout = jnp.concatenate(blocks_of_ctx(layout), 0)
    grad_blocks = blocks_of_ctx(after(own_grads, inputs))
    seq = layout[:, 0].reshape(-1)
    pos = layout[:, 1].reshape(-1)

    inputs, out = lax.optimization_barrier((inputs, out))
    normed, inv_std = normalize(inputs.astype(f32))
    first_in = (normed * gain_one + bias_one).astype(bf16)
    second_in = (normed * gain_two + bias_two).astype(bf16)

    projected = jnp.dot(first_in, qkv, preferred_element_type=f32)
    projected = projected.reshape(total_rows, 3, heads, HEAD_DIM)
    cosines, sines = rotary_tables(pos)
    queries = rotate(projected[:, 0], cosines, sines).astype(bf16)
    keys = rotate(projected[:, 1], cosines, sines).astype(bf16)
    values = projected[:, 2].astype(bf16)
    scores = jnp.einsum("qhd,khd->hqk", queries, keys, preferred_element_type=f32) * scale
    allowed = ((seq[:, None] == seq[None, :]) & (pos[None, :] <= pos[:, None]))[None]
    masked = jnp.where(allowed, scores, NEG_FILL)
    row_max = jnp.max(masked, axis=-1, keepdims=True)
    weights = jnp.where(allowed, jnp.exp(masked - row_max), 0.0)
    row_total = jnp.sum(weights, axis=-1, keepdims=True)
    weights = weights / row_total
    weights_low = weights.astype(bf16)
    attended = jnp.einsum("hqk,khd->qhd", weights_low, values, preferred_element_type=f32)
    attended_low = attended.reshape(total_rows, heads * HEAD_DIM).astype(bf16)

    grads = jnp.concatenate(after(grad_blocks, attended_low), 0)
    grad_attended = lax.dot_general(grads, out, COLS_BOTH, preferred_element_type=f32)
    grad_attended = grad_attended.reshape(total_rows, heads, HEAD_DIM)
    delta = jnp.sum(grad_attended * attended, axis=-1).T[..., None]
    grad_heads = grad_attended.astype(bf16)
    grad_values = jnp.einsum("hqk,qhd->khd", weights_low, grad_heads, preferred_element_type=f32)
    grad_weights = jnp.einsum("qhd,khd->hqk", grad_heads, values, preferred_element_type=f32)
    grad_scores = (weights * (grad_weights - delta)).astype(bf16)
    grad_queries = (
        jnp.einsum("hqk,khd->qhd", grad_scores, keys, preferred_element_type=f32) * scale
    )
    grad_keys = jnp.einsum("hqk,qhd->khd", grad_scores, queries, preferred_element_type=f32) * scale
    grad_projected = jnp.stack(
        [
            rotate(grad_queries, cosines, -sines),
            rotate(grad_keys, cosines, -sines),
            grad_values,
        ],
        1,
    )
    grad_projected = grad_projected.reshape(total_rows, 3 * heads * HEAD_DIM).astype(bf16)
    pair_qkv = sum_pair(first_in, grad_projected)
    pair_out = sum_pair(attended_low, grads)
    lines = lax.axis_size("line")
    pair_attn = jnp.concatenate([pair_qkv, fold(pair_out, lines, ctx_count)], 1)
    summed_attn = sum_rows(pair_attn)
    mlp = after(mlp, pair_attn)
    half = mlp.shape[1] // 2
    up = mlp[:, :half]

    hidden_pre = jnp.dot(second_in, up, preferred_element_type=f32)
    below = 0.5 + 0.5 * lax.erf(hidden_pre * (0.5**0.5))
    bell = jnp.exp(-0.5 * hidden_pre * hidden_pre) * (0.5 / jnp.pi) ** 0.5
    active = (hidden_pre * below).astype(bf16)
    slope = below + hidden_pre * bell
    activated, slope = lax.optimization_barrier((active, slope))
    pair_down = sum_pair(grads, activated)
    ready_down = return_early(pair_down)
    mlp = after(mlp, pair_down)
    grad_act = jnp.dot(grads, mlp[:, half:], preferred_element_type=f32)
    grad_hidden = (grad_act * slope).astype(bf16)
    pair_up = sum_pair(second_in, grad_hidden)
    summed_up = sum_rows(pair_up)
    mlp, qkv, out = lax.optimization_barrier((mlp, qkv, out, pair_up))[:3]
    branches = jnp.dot(attended_low, out, preferred_element_type=f32)
    down_part = lax.dot_general(
        activated, mlp[:, half:], COLS_BOTH, preferred_element_type=f32
    )
    branches = (branches + down_part).astype(bf16)
    mlp, qkv = lax.optimization_barrier((mlp, qkv, branches))[:2]
    grad_second = lax.dot_general(grad_hidden, mlp[:, :half], COLS_BOTH, preferred_element_type=f32)
    grad_first = lax.dot_general(grad_projected, qkv, COLS_BOTH, preferred_element_type=f32)
    scaled = (grad_first * gain_one + grad_second * gain_two).astype(bf16)
    grad_first, grad_second, scaled = lax.optimization_barrier((grad_first, grad_second, scaled))
    ready_down = after(ready_down, scaled).swapaxes(0, 1).reshape(pair_down.shape)
    summed_down = sum_rows(ready_down)
    output = scatter_ctx(branches, rows, ready_down) + own_tokens.astype(f32)
    output = outer(output.astype(bf16))[None]
    norm_terms = jnp.stack(
        [
            jnp.sum(grad_first * normed, 0),
            jnp.sum(grad_first, 0),
            jnp.sum(grad_second * normed, 0),
            jnp.sum(grad_second, 0),
        ]
    )
    summed_attn = after(summed_attn, norm_terms)
    summed_qkv = summed_attn[:, : mine_qkv.shape[1]]
    summed_out = unfold(summed_attn[:, mine_qkv.shape[1] :], 1, ctx_count)
    summed_up = after(summed_up, norm_terms)
    scaled = scatter_ctx(scaled, rows, norm_terms)
    norm_terms = norm_terms.reshape(4, fsdp_count, ctx_count, -1).transpose(2, 1, 0, 3)
    norm_terms = norm_terms.reshape(ctx_count * fsdp_count, -1)
    norm_sums = lax.all_to_all(norm_terms, ("ctx", *FSDP), 0, 0, tiled=True)
    norm_sums = jnp.sum(norm_sums, 0).reshape(4, -1)

    own_normed = normed[:rows]
    first_mean = jnp.mean(scaled, axis=-1, keepdims=True)
    second_mean = jnp.mean(scaled * own_normed, axis=-1, keepdims=True)
    back = (scaled - first_mean - own_normed * second_mean) * inv_std[:rows]
    grad_tokens = outer((own_grads.astype(f32) + back).astype(bf16))[None]
    return (
        output,
        grad_tokens,
        norm_sums[0],
        norm_sums[1],
        norm_sums[2],
        norm_sums[3],
        return_columns(summed_qkv, 3, grad_tokens),
        outer(summed_out.astype(f32)),
        return_columns(summed_up, 1, grad_tokens),
        row_shard(summed_down.reshape(ctx_count, -1, summed_down.shape[1]), 1),
    )


def solution(mesh):
    shape = (mesh.shape["ctx"], mesh.shape["fsdp"] // CORES, CORES)
    split = Mesh(np.asarray(mesh.devices).reshape(shape), ("ctx", *FSDP))
    blocks = P(FSDP, "ctx", None)
    ids = P(FSDP, "ctx")
    shards = P(("ctx", *FSDP), None)
    vector = P(("ctx", *FSDP))

    return jax.shard_map(
        on_device,
        mesh=split,
        in_specs=(blocks, ids, ids, P(), P(), P(), P(), shards, shards, shards, shards, blocks),
        out_specs=(blocks, blocks, vector, vector, vector, vector, shards, shards, shards, shards),
        check_vma=False,
    )
```

```python
import jax
import jax.numpy as jnp
import numpy as np
from jax import lax
from jax.sharding import Mesh
from jax.sharding import PartitionSpec as P

HEADS = 8
HEAD_DIM = 256
ROT = 64


NORM_EPS = 1e-05
NEG_FILL = -1e30
ROPE_BASE = 10000.0
CORES = 2
FSDP = ("line", "core")
ROWS_FIRST = (((0,), (0,)), ((), ()))
COLS_BOTH = (((1,), (1,)), ((), ()))


def swap(value, step):
    count = lax.axis_size("ctx")
    return lax.ppermute(value, "ctx", [(i, i ^ step) for i in range(count)])


def blocks_of_ctx(block):
    count = lax.axis_size("ctx")
    return (block, *(swap(block, k) for k in range(1, count)))


def scatter_ctx(low, rows, until):
    count = lax.axis_size("ctx")
    came = [swap(low[k * rows : (k + 1) * rows], k) for k in range(1, count)]
    came = after(tuple(came), until)
    total = low[:rows].astype(jnp.float32)
    for part in came:
        total = total + part.astype(jnp.float32)
    return total


def turn(value, first, second):
    lead, width = value.shape[:-1], value.shape[-1]
    split = value.reshape(*lead, first, second, width // (first * second))
    return jnp.swapaxes(split, -3, -2).reshape(*lead, width)


def normalize(inputs):
    row_mean = jnp.mean(inputs, axis=-1, keepdims=True)
    centred = inputs - row_mean
    inv_std = lax.rsqrt(jnp.mean(centred * centred, axis=-1, keepdims=True) + NORM_EPS)
    return (centred * inv_std, inv_std)


def rotary_tables(position_row):
    half_dims = ROT // 2
    freqs = ROPE_BASE ** (-(jnp.arange(half_dims, dtype=jnp.float32) * 2.0) / ROT)
    angles = position_row.astype(jnp.float32)[:, None] * freqs[None, :]
    cosines = jnp.cos(angles)
    sines = jnp.sin(angles)
    return (
        jnp.concatenate([cosines, cosines], -1)[:, None, :],
        jnp.concatenate([sines, sines], -1)[:, None, :],
    )


def rotate(heads, cosines, sines):
    half_dims = ROT // 2
    turned = heads[..., :ROT]
    swapped = jnp.concatenate([-turned[..., half_dims:], turned[..., :half_dims]], -1)
    return jnp.concatenate([turned * cosines + swapped * sines, heads[..., ROT:]], -1)


def after(value, earlier):
    return value if earlier is None else lax.optimization_barrier((value, earlier))[0]


def exchange_columns(shard, groups, earlier=None):
    count = lax.axis_size("ctx")
    rows, columns = shard.shape
    split = shard.reshape(rows, groups, count, columns // (groups * count)).transpose(2, 0, 1, 3)
    split = after(split.reshape(count, rows, columns // count), earlier)
    mine = lax.all_to_all(split, "ctx", 0, 0, tiled=True)
    return mine.reshape(count * rows, columns // count)


def gather_rows(mine):
    return lax.all_gather(mine, FSDP, axis=0, tiled=True)


def gather_small(mine):
    lines, core, line = lax.axis_size("line"), lax.axis_index("core"), lax.axis_index("line")
    came = [lax.ppermute(mine, "line", [(i, i ^ k) for i in range(lines)]) for k in range(1, lines)]
    same = jnp.stack([mine, *came])
    other = lax.ppermute(same, "core", [(0, 1), (1, 0)])
    both = jnp.stack([jnp.where(core == 0, same, other), jnp.where(core == 0, other, same)], 1)
    rows = [lax.dynamic_index_in_dim(both, line ^ k, 0, keepdims=False) for k in range(lines)]
    return jnp.stack(rows).reshape(-1, mine.shape[1])


def sum_pair(left, right):
    core = lax.axis_index("core")
    grad = lax.dot_general(left, right, ROWS_FIRST, preferred_element_type=jnp.float32)
    blocks = grad.astype(jnp.bfloat16).reshape(lax.axis_size("line"), CORES, -1, grad.shape[1])
    sent = lax.dynamic_index_in_dim(blocks, CORES - 1 - core, 1, keepdims=False)
    came = lax.ppermute(sent, "core", [(0, 1), (1, 0)])
    kept = lax.dynamic_index_in_dim(blocks, core, 1, keepdims=False)
    pair = kept.astype(jnp.float32) + came.astype(jnp.float32)
    return pair.astype(jnp.bfloat16).reshape(-1, grad.shape[1])


def sum_rows(pair):
    return lax.psum_scatter(pair, "line", scatter_dimension=0, tiled=True)


def fold(value, blocks, count):
    rows, columns = value.shape
    split = value.reshape(blocks, rows // blocks, count, columns // count)
    return jnp.swapaxes(split, 1, 2).reshape(rows * count, columns // count)


def unfold(value, blocks, count):
    rows, columns = value.shape
    split = value.reshape(blocks, count, rows // (blocks * count), columns)
    return jnp.swapaxes(split, 1, 2).reshape(rows // count, columns * count)


def return_columns(summed, groups, until):
    count = lax.axis_size("ctx")
    split = summed.reshape(count, summed.shape[0] // count, summed.shape[1])
    mine = lax.all_to_all(split, "ctx", 0, 0, tiled=True)
    return row_shard(after(mine, until), groups)


def return_early(pair):
    count, lines = lax.axis_size("ctx"), lax.axis_size("line")
    split = pair.reshape(lines, count, -1, pair.shape[1]).swapaxes(0, 1)
    return lax.all_to_all(split, "ctx", 0, 0, tiled=True)


def row_shard(mine, groups):
    if groups > 1:
        split = mine.reshape(*mine.shape[:2], groups, -1).transpose(1, 2, 0, 3)
        return split.reshape(mine.shape[1], -1).astype(jnp.float32)
    part = mine.shape[2] // groups
    pieces = [
        mine[c, :, g * part : (g + 1) * part] for g in range(groups) for c in range(mine.shape[0])
    ]
    return jnp.concatenate(pieces, 1).astype(jnp.float32)


def on_device(
    tokens,
    seq_ids,
    positions,
    ln1_gain,
    ln1_bias,
    ln2_gain,
    ln2_bias,
    w_qkv,
    w_out,
    w_up,
    w_down,
    grad_out,
):
    f32 = jnp.float32
    bf16 = jnp.bfloat16
    rows = tokens.shape[1]
    ctx_count = lax.axis_size("ctx")
    fsdp_count = lax.axis_size("line") * CORES
    heads = HEADS // ctx_count
    total_rows = rows * ctx_count
    scale = HEAD_DIM ** (-0.5)

    def inner(value):
        return turn(value, ctx_count, fsdp_count)

    def outer(value):
        return turn(value, fsdp_count, ctx_count)

    out = inner(gather_small(w_out))
    mine_qkv = exchange_columns(w_qkv, 3)
    qkv = gather_rows(mine_qkv)
    mine_mlp = exchange_columns(jnp.concatenate([w_up, w_down], 1), 2, mine_qkv)
    mlp = gather_rows(mine_mlp)

    gain_one = inner(ln1_gain.astype(f32))
    bias_one = inner(ln1_bias.astype(f32))
    gain_two = inner(ln2_gain.astype(f32))
    bias_two = inner(ln2_bias.astype(f32))
    own_tokens = inner(tokens[0])
    own_grads = inner(grad_out[0])
    inputs = jnp.concatenate(blocks_of_ctx(after(own_tokens, mine_mlp)), 0)
    layout = after(jnp.stack([seq_ids[0], positions[0]], 0)[None], mine_mlp)
    layout = jnp.concatenate(blocks_of_ctx(layout), 0)
    grad_blocks = blocks_of_ctx(after(own_grads, inputs))
    seq = layout[:, 0].reshape(-1)
    pos = layout[:, 1].reshape(-1)

    inputs, out = lax.optimization_barrier((inputs, out))
    normed, inv_std = normalize(inputs.astype(f32))
    first_in = (normed * gain_one + bias_one).astype(bf16)
    second_in = (normed * gain_two + bias_two).astype(bf16)

    projected = jnp.dot(first_in, qkv, preferred_element_type=f32)
    projected = projected.reshape(total_rows, 3, heads, HEAD_DIM)
    cosines, sines = rotary_tables(pos)
    queries = rotate(projected[:, 0], cosines, sines).astype(bf16)
    keys = rotate(projected[:, 1], cosines, sines).astype(bf16)
    values = projected[:, 2].astype(bf16)
    scores = jnp.einsum("qhd,khd->hqk", queries, keys, preferred_element_type=f32) * scale
    allowed = ((seq[:, None] == seq[None, :]) & (pos[None, :] <= pos[:, None]))[None]
    masked = jnp.where(allowed, scores, NEG_FILL)
    row_max = jnp.max(masked, axis=-1, keepdims=True)
    weights = jnp.where(allowed, jnp.exp(masked - row_max), 0.0)
    row_total = jnp.sum(weights, axis=-1, keepdims=True)
    weights = weights / row_total
    weights_low = weights.astype(bf16)
    attended = jnp.einsum("hqk,khd->qhd", weights_low, values, preferred_element_type=f32)
    attended_low = attended.reshape(total_rows, heads * HEAD_DIM).astype(bf16)

    grads = jnp.concatenate(after(grad_blocks, attended_low), 0)
    grad_attended = lax.dot_general(grads, out, COLS_BOTH, preferred_element_type=f32)
    grad_attended = grad_attended.reshape(total_rows, heads, HEAD_DIM)
    delta = jnp.sum(grad_attended * attended, axis=-1).T[..., None]
    grad_heads = grad_attended.astype(bf16)
    grad_values = jnp.einsum("hqk,qhd->khd", weights_low, grad_heads, preferred_element_type=f32)
    grad_weights = jnp.einsum("qhd,khd->hqk", grad_heads, values, preferred_element_type=f32)
    grad_scores = (weights * (grad_weights - delta)).astype(bf16)
    grad_queries = (
        jnp.einsum("hqk,khd->qhd", grad_scores, keys, preferred_element_type=f32) * scale
    )
    grad_keys = jnp.einsum("hqk,qhd->khd", grad_scores, queries, preferred_element_type=f32) * scale
    grad_projected = jnp.stack(
        [
            rotate(grad_queries, cosines, -sines),
            rotate(grad_keys, cosines, -sines),
            grad_values,
        ],
        1,
    )
    grad_projected = grad_projected.reshape(total_rows, 3 * heads * HEAD_DIM).astype(bf16)
    pair_qkv = sum_pair(first_in, grad_projected)
    pair_out = sum_pair(attended_low, grads)
    lines = lax.axis_size("line")
    pair_attn = jnp.concatenate([pair_qkv, fold(pair_out, lines, ctx_count)], 1)
    summed_attn = sum_rows(pair_attn)
    mlp = after(mlp, pair_attn)
    half = mlp.shape[1] // 2
    up = mlp[:, :half]

    hidden_pre = jnp.dot(second_in, up, preferred_element_type=f32)
    below = 0.5 + 0.5 * lax.erf(hidden_pre * (0.5**0.5))
    bell = jnp.exp(-0.5 * hidden_pre * hidden_pre) * (0.5 / jnp.pi) ** 0.5
    active = (hidden_pre * below).astype(bf16)
    slope = below + hidden_pre * bell
    activated, slope = lax.optimization_barrier((active, slope))
    pair_down = sum_pair(grads, activated)
    ready_down = return_early(pair_down)
    mlp = after(mlp, pair_down)
    grad_act = jnp.dot(grads, mlp[:, half:], preferred_element_type=f32)
    grad_hidden = (grad_act * slope).astype(bf16)
    pair_up = sum_pair(second_in, grad_hidden)
    summed_up = sum_rows(pair_up)
    mlp, qkv, out = lax.optimization_barrier((mlp, qkv, out, pair_up))[:3]
    branches = jnp.dot(attended_low, out, preferred_element_type=f32)
    down_part = lax.dot_general(
        activated, mlp[:, half:], COLS_BOTH, preferred_element_type=f32
    )
    branches = (branches + down_part).astype(bf16)
    mlp, qkv = lax.optimization_barrier((mlp, qkv, branches))[:2]
    grad_second = lax.dot_general(grad_hidden, mlp[:, :half], COLS_BOTH, preferred_element_type=f32)
    grad_first = lax.dot_general(grad_projected, qkv, COLS_BOTH, preferred_element_type=f32)
    scaled = (grad_first * gain_one + grad_second * gain_two).astype(bf16)
    grad_first, grad_second, scaled = lax.optimization_barrier((grad_first, grad_second, scaled))
    ready_down = after(ready_down, scaled).swapaxes(0, 1).reshape(pair_down.shape)
    summed_down = sum_rows(ready_down)
    output = scatter_ctx(branches, rows, ready_down) + own_tokens.astype(f32)
    output = outer(output.astype(bf16))[None]
    norm_terms = jnp.stack(
        [
            jnp.sum(grad_first * normed, 0),
            jnp.sum(grad_first, 0),
            jnp.sum(grad_second * normed, 0),
            jnp.sum(grad_second, 0),
        ]
    )
    summed_attn = after(summed_attn, norm_terms)
    summed_qkv = summed_attn[:, : mine_qkv.shape[1]]
    summed_out = unfold(summed_attn[:, mine_qkv.shape[1] :], 1, ctx_count)
    summed_up = after(summed_up, norm_terms)
    scaled = scatter_ctx(scaled, rows, norm_terms)
    norm_terms = norm_terms.reshape(4, fsdp_count, ctx_count, -1).transpose(2, 1, 0, 3)
    norm_terms = norm_terms.reshape(ctx_count * fsdp_count, -1)
    norm_sums = lax.all_to_all(norm_terms, ("ctx", *FSDP), 0, 0, tiled=True)
    norm_sums = jnp.sum(norm_sums, 0).reshape(4, -1)

    own_normed = normed[:rows]
    first_mean = jnp.mean(scaled, axis=-1, keepdims=True)
    second_mean = jnp.mean(scaled * own_normed, axis=-1, keepdims=True)
    back = (scaled - first_mean - own_normed * second_mean) * inv_std[:rows]
    grad_tokens = outer((own_grads.astype(f32) + back).astype(bf16))[None]
    return (
        output,
        grad_tokens,
        norm_sums[0],
        norm_sums[1],
        norm_sums[2],
        norm_sums[3],
        return_columns(summed_qkv, 3, grad_tokens),
        outer(summed_out.astype(f32)),
        return_columns(summed_up, 1, grad_tokens),
        row_shard(summed_down.reshape(ctx_count, -1, summed_down.shape[1]), 1),
    )


def solution(mesh):
    shape = (mesh.shape["ctx"], mesh.shape["fsdp"] // CORES, CORES)
    split = Mesh(np.asarray(mesh.devices).reshape(shape), ("ctx", *FSDP))
    blocks = P(FSDP, "ctx", None)
    ids = P(FSDP, "ctx")
    shards = P(("ctx", *FSDP), None)
    vector = P(("ctx", *FSDP))

    return jax.shard_map(
        on_device,
        mesh=split,
        in_specs=(blocks, ids, ids, P(), P(), P(), P(), shards, shards, shards, shards, blocks),
        out_specs=(blocks, blocks, vector, vector, vector, vector, shards, shards, shards, shards),
        check_vma=False,
    )
```

```python
import jax
import jax.numpy as jnp
import numpy as np
from jax import lax
from jax.sharding import Mesh
from jax.sharding import PartitionSpec as P

HEADS = 8
HEAD_DIM = 256
ROT = 64


NORM_EPS = 1e-05
NEG_FILL = -1e30
ROPE_BASE = 10000.0
CORES = 2
FSDP = ("line", "core")
ROWS_FIRST = (((0,), (0,)), ((), ()))
COLS_BOTH = (((1,), (1,)), ((), ()))


def swap(value, step):
    count = lax.axis_size("ctx")
    return lax.ppermute(value, "ctx", [(i, i ^ step) for i in range(count)])


def blocks_of_ctx(block):
    count = lax.axis_size("ctx")
    return (block, *(swap(block, k) for k in range(1, count)))


def scatter_ctx(low, rows, until):
    count = lax.axis_size("ctx")
    came = [swap(low[k * rows : (k + 1) * rows], k) for k in range(1, count)]
    came = after(tuple(came), until)
    total = low[:rows].astype(jnp.float32)
    for part in came:
        total = total + part.astype(jnp.float32)
    return total


def turn(value, first, second):
    lead, width = value.shape[:-1], value.shape[-1]
    split = value.reshape(*lead, first, second, width // (first * second))
    return jnp.swapaxes(split, -3, -2).reshape(*lead, width)


def normalize(inputs):
    row_mean = jnp.mean(inputs, axis=-1, keepdims=True)
    centred = inputs - row_mean
    inv_std = lax.rsqrt(jnp.mean(centred * centred, axis=-1, keepdims=True) + NORM_EPS)
    return (centred * inv_std, inv_std)


def rotary_tables(position_row):
    half_dims = ROT // 2
    freqs = ROPE_BASE ** (-(jnp.arange(half_dims, dtype=jnp.float32) * 2.0) / ROT)
    angles = position_row.astype(jnp.float32)[:, None] * freqs[None, :]
    cosines = jnp.cos(angles)
    sines = jnp.sin(angles)
    return (
        jnp.concatenate([cosines, cosines], -1)[:, None, :],
        jnp.concatenate([sines, sines], -1)[:, None, :],
    )


def rotate(heads, cosines, sines):
    half_dims = ROT // 2
    turned = heads[..., :ROT]
    swapped = jnp.concatenate([-turned[..., half_dims:], turned[..., :half_dims]], -1)
    return jnp.concatenate([turned * cosines + swapped * sines, heads[..., ROT:]], -1)


def after(value, earlier):
    return value if earlier is None else lax.optimization_barrier((value, earlier))[0]


def exchange_columns(shard, groups, earlier=None):
    count = lax.axis_size("ctx")
    rows, columns = shard.shape
    split = shard.reshape(rows, groups, count, columns // (groups * count)).transpose(2, 0, 1, 3)
    split = after(split.reshape(count, rows, columns // count), earlier)
    mine = lax.all_to_all(split, "ctx", 0, 0, tiled=True)
    return mine.reshape(count * rows, columns // count)


def gather_rows(mine):
    return lax.all_gather(mine, FSDP, axis=0, tiled=True)


def gather_small(mine):
    lines, core, line = lax.axis_size("line"), lax.axis_index("core"), lax.axis_index("line")
    came = [lax.ppermute(mine, "line", [(i, i ^ k) for i in range(lines)]) for k in range(1, lines)]
    same = jnp.stack([mine, *came])
    other = lax.ppermute(same, "core", [(0, 1), (1, 0)])
    both = jnp.stack([jnp.where(core == 0, same, other), jnp.where(core == 0, other, same)], 1)
    rows = [lax.dynamic_index_in_dim(both, line ^ k, 0, keepdims=False) for k in range(lines)]
    return jnp.stack(rows).reshape(-1, mine.shape[1])


def sum_pair(left, right):
    core = lax.axis_index("core")
    grad = lax.dot_general(left, right, ROWS_FIRST, preferred_element_type=jnp.float32)
    blocks = grad.astype(jnp.bfloat16).reshape(lax.axis_size("line"), CORES, -1, grad.shape[1])
    sent = lax.dynamic_index_in_dim(blocks, CORES - 1 - core, 1, keepdims=False)
    came = lax.ppermute(sent, "core", [(0, 1), (1, 0)])
    kept = lax.dynamic_index_in_dim(blocks, core, 1, keepdims=False)
    pair = kept.astype(jnp.float32) + came.astype(jnp.float32)
    return pair.astype(jnp.bfloat16).reshape(-1, grad.shape[1])


def sum_rows(pair):
    return lax.psum_scatter(pair, "line", scatter_dimension=0, tiled=True)


def fold(value, blocks, count):
    rows, columns = value.shape
    split = value.reshape(blocks, rows // blocks, count, columns // count)
    return jnp.swapaxes(split, 1, 2).reshape(rows * count, columns // count)


def unfold(value, blocks, count):
    rows, columns = value.shape
    split = value.reshape(blocks, count, rows // (blocks * count), columns)
    return jnp.swapaxes(split, 1, 2).reshape(rows // count, columns * count)


def return_columns(summed, groups, until):
    count = lax.axis_size("ctx")
    split = summed.reshape(count, summed.shape[0] // count, summed.shape[1])
    mine = lax.all_to_all(split, "ctx", 0, 0, tiled=True)
    return row_shard(after(mine, until), groups)


def return_early(pair):
    count, lines = lax.axis_size("ctx"), lax.axis_size("line")
    split = pair.reshape(lines, count, -1, pair.shape[1]).swapaxes(0, 1)
    return lax.all_to_all(split, "ctx", 0, 0, tiled=True)


def row_shard(mine, groups):
    if groups > 1:
        split = mine.reshape(*mine.shape[:2], groups, -1).transpose(1, 2, 0, 3)
        return split.reshape(mine.shape[1], -1).astype(jnp.float32)
    part = mine.shape[2] // groups
    pieces = [
        mine[c, :, g * part : (g + 1) * part] for g in range(groups) for c in range(mine.shape[0])
    ]
    return jnp.concatenate(pieces, 1).astype(jnp.float32)


def on_device(
    tokens,
    seq_ids,
    positions,
    ln1_gain,
    ln1_bias,
    ln2_gain,
    ln2_bias,
    w_qkv,
    w_out,
    w_up,
    w_down,
    grad_out,
):
    f32 = jnp.float32
    bf16 = jnp.bfloat16
    rows = tokens.shape[1]
    ctx_count = lax.axis_size("ctx")
    fsdp_count = lax.axis_size("line") * CORES
    heads = HEADS // ctx_count
    total_rows = rows * ctx_count
    scale = HEAD_DIM ** (-0.5)

    def inner(value):
        return turn(value, ctx_count, fsdp_count)

    def outer(value):
        return turn(value, fsdp_count, ctx_count)

    out = inner(gather_small(w_out))
    mine_qkv = exchange_columns(w_qkv, 3)
    qkv = gather_rows(mine_qkv)
    mine_mlp = exchange_columns(jnp.concatenate([w_up, w_down], 1), 2, mine_qkv)
    mlp = gather_rows(mine_mlp)

    gain_one = inner(ln1_gain.astype(f32))
    bias_one = inner(ln1_bias.astype(f32))
    gain_two = inner(ln2_gain.astype(f32))
    bias_two = inner(ln2_bias.astype(f32))
    own_tokens = inner(tokens[0])
    own_grads = inner(grad_out[0])
    inputs = jnp.concatenate(blocks_of_ctx(after(own_tokens, mine_mlp)), 0)
    layout = after(jnp.stack([seq_ids[0], positions[0]], 0)[None], mine_mlp)
    layout = jnp.concatenate(blocks_of_ctx(layout), 0)
    grad_blocks = blocks_of_ctx(after(own_grads, inputs))
    seq = layout[:, 0].reshape(-1)
    pos = layout[:, 1].reshape(-1)

    inputs, out = lax.optimization_barrier((inputs, out))
    normed, inv_std = normalize(inputs.astype(f32))
    first_in = (normed * gain_one + bias_one).astype(bf16)
    second_in = (normed * gain_two + bias_two).astype(bf16)

    projected = jnp.dot(first_in, qkv, preferred_element_type=f32)
    projected = projected.reshape(total_rows, 3, heads, HEAD_DIM)
    cosines, sines = rotary_tables(pos)
    queries = rotate(projected[:, 0], cosines, sines).astype(bf16)
    keys = rotate(projected[:, 1], cosines, sines).astype(bf16)
    values = projected[:, 2].astype(bf16)
    scores = jnp.einsum("qhd,khd->hqk", queries, keys, preferred_element_type=f32) * scale
    allowed = ((seq[:, None] == seq[None, :]) & (pos[None, :] <= pos[:, None]))[None]
    masked = jnp.where(allowed, scores, NEG_FILL)
    row_max = jnp.max(masked, axis=-1, keepdims=True)
    weights = jnp.where(allowed, jnp.exp(masked - row_max), 0.0)
    row_total = jnp.sum(weights, axis=-1, keepdims=True)
    weights = weights / row_total
    weights_low = weights.astype(bf16)
    attended = jnp.einsum("hqk,khd->qhd", weights_low, values, preferred_element_type=f32)
    attended_low = attended.reshape(total_rows, heads * HEAD_DIM).astype(bf16)

    grads = jnp.concatenate(after(grad_blocks, attended_low), 0)
    grad_attended = lax.dot_general(grads, out, COLS_BOTH, preferred_element_type=f32)
    grad_attended = grad_attended.reshape(total_rows, heads, HEAD_DIM)
    delta = jnp.sum(grad_attended * attended, axis=-1).T[..., None]
    grad_heads = grad_attended.astype(bf16)
    grad_values = jnp.einsum("hqk,qhd->khd", weights_low, grad_heads, preferred_element_type=f32)
    grad_weights = jnp.einsum("qhd,khd->hqk", grad_heads, values, preferred_element_type=f32)
    grad_scores = (weights * (grad_weights - delta)).astype(bf16)
    grad_queries = (
        jnp.einsum("hqk,khd->qhd", grad_scores, keys, preferred_element_type=f32) * scale
    )
    grad_keys = jnp.einsum("hqk,qhd->khd", grad_scores, queries, preferred_element_type=f32) * scale
    grad_projected = jnp.stack(
        [
            rotate(grad_queries, cosines, -sines),
            rotate(grad_keys, cosines, -sines),
            grad_values,
        ],
        1,
    )
    grad_projected = grad_projected.reshape(total_rows, 3 * heads * HEAD_DIM).astype(bf16)
    pair_qkv = sum_pair(first_in, grad_projected)
    pair_out = sum_pair(attended_low, grads)
    lines = lax.axis_size("line")
    pair_attn = jnp.concatenate([pair_qkv, fold(pair_out, lines, ctx_count)], 1)
    summed_attn = sum_rows(pair_attn)
    mlp = after(mlp, pair_attn)
    half = mlp.shape[1] // 2
    up = mlp[:, :half]

    hidden_pre = jnp.dot(second_in, up, preferred_element_type=f32)
    below = 0.5 + 0.5 * lax.erf(hidden_pre * (0.5**0.5))
    bell = jnp.exp(-0.5 * hidden_pre * hidden_pre) * (0.5 / jnp.pi) ** 0.5
    active = (hidden_pre * below).astype(bf16)
    slope = below + hidden_pre * bell
    activated, slope = lax.optimization_barrier((active, slope))
    pair_down = sum_pair(grads, activated)
    ready_down = return_early(pair_down)
    mlp = after(mlp, pair_down)
    grad_act = jnp.dot(grads, mlp[:, half:], preferred_element_type=f32)
    grad_hidden = (grad_act * slope).astype(bf16)
    pair_up = sum_pair(second_in, grad_hidden)
    summed_up = sum_rows(pair_up)
    mlp, qkv, out = lax.optimization_barrier((mlp, qkv, out, pair_up))[:3]
    branches = jnp.dot(attended_low, out, preferred_element_type=f32)
    down_part = lax.dot_general(
        activated, mlp[:, half:], COLS_BOTH, preferred_element_type=f32
    )
    branches = (branches + down_part).astype(bf16)
    mlp, qkv = lax.optimization_barrier((mlp, qkv, branches))[:2]
    grad_second = lax.dot_general(grad_hidden, mlp[:, :half], COLS_BOTH, preferred_element_type=f32)
    grad_first = lax.dot_general(grad_projected, qkv, COLS_BOTH, preferred_element_type=f32)
    scaled = (grad_first * gain_one + grad_second * gain_two).astype(bf16)
    grad_first, grad_second, scaled = lax.optimization_barrier((grad_first, grad_second, scaled))
    ready_down = after(ready_down, scaled).transpose(1, 2, 0, 3)
    ready_down = ready_down.reshape(-1, ctx_count * pair_down.shape[1])
    summed_down = sum_rows(ready_down)
    output = scatter_ctx(branches, rows, ready_down) + own_tokens.astype(f32)
    output = outer(output.astype(bf16))[None]
    norm_terms = jnp.stack(
        [
            jnp.sum(grad_first * normed, 0),
            jnp.sum(grad_first, 0),
            jnp.sum(grad_second * normed, 0),
            jnp.sum(grad_second, 0),
        ]
    )
    summed_attn = after(summed_attn, norm_terms)
    summed_qkv = summed_attn[:, : mine_qkv.shape[1]]
    summed_out = unfold(summed_attn[:, mine_qkv.shape[1] :], 1, ctx_count)
    summed_up = after(summed_up, norm_terms)
    scaled = scatter_ctx(scaled, rows, norm_terms)
    norm_terms = norm_terms.reshape(4, fsdp_count, ctx_count, -1).transpose(2, 1, 0, 3)
    norm_terms = norm_terms.reshape(ctx_count * fsdp_count, -1)
    norm_sums = lax.all_to_all(norm_terms, ("ctx", *FSDP), 0, 0, tiled=True)
    norm_sums = jnp.sum(norm_sums, 0).reshape(4, -1)

    own_normed = normed[:rows]
    first_mean = jnp.mean(scaled, axis=-1, keepdims=True)
    second_mean = jnp.mean(scaled * own_normed, axis=-1, keepdims=True)
    back = (scaled - first_mean - own_normed * second_mean) * inv_std[:rows]
    grad_tokens = outer((own_grads.astype(f32) + back).astype(bf16))[None]
    grad_up = return_columns(summed_up, 1, grad_tokens)
    return (
        output,
        grad_tokens,
        norm_sums[0],
        norm_sums[1],
        norm_sums[2],
        norm_sums[3],
        return_columns(summed_qkv, 3, grad_tokens),
        outer(summed_out.astype(f32)),
        grad_up,
        summed_down.astype(f32),
    )


def solution(mesh):
    shape = (mesh.shape["ctx"], mesh.shape["fsdp"] // CORES, CORES)
    split = Mesh(np.asarray(mesh.devices).reshape(shape), ("ctx", *FSDP))
    blocks = P(FSDP, "ctx", None)
    ids = P(FSDP, "ctx")
    shards = P(("ctx", *FSDP), None)
    vector = P(("ctx", *FSDP))

    return jax.shard_map(
        on_device,
        mesh=split,
        in_specs=(blocks, ids, ids, P(), P(), P(), P(), shards, shards, shards, shards, blocks),
        out_specs=(blocks, blocks, vector, vector, vector, vector, shards, shards, shards, shards),
        check_vma=False,
    )
```
